32 devices in a mesh: region: 16 (over z, y, core), freq: 2 (over x).
Axes of the slice: x: 2, y: 2, z: 4, core: 2. Of those that a mesh axis runs over, the one named last changes fastest.
Arguments:
- dirty_map: float32 [4, 16384], P('freq', 'region'), may hold values from -6 to 6
- psf_blocks: bfloat16 [4, 128, 7, 128, 128], P('freq', 'region'), as said below
- col_index: int32 [128, 7], P('region'), may hold values from 0 to 127, as said below
- block_live: int32 [128, 7], P('region'), may hold values from 0 to 1, as said below
Outputs:
- source_map: float32 [4, 16384], P('freq', 'region')
- broadband: float32 [16384], P('region')
The draws below stay inside these ranges and needn't reach their ends.
Inputs may be any that keep to these rules, and one draw needn't show every extreme that they name: `col_index`: block row i stores itself in slot 0; the pattern is symmetric: if row i names j then row j names i, and column offsets are the same for every row (mod 128). `block_live`: slot 0 is always 1; the flag of block (i, j) equals that of block (j, i). `psf_blocks`: the operator is symmetric: the block of row i naming column j is the transpose of the block of row j naming column i; diagonal entries of slot 0 lie between 0.9 and 1.1.
All inputs are finite; a program needn't handle non-finite values.
Results may differ from the reference program's by a relative error of at most 0.0032.
Values may be sent and summed in bfloat16 or wider, within the bound.
A program may use at most 64 MiB of HBM per device.

```python
import math
import jax
import jax.numpy as jnp
from jax import lax

BS = 128
K = 7
BR = 8
ITERS = 3
NBLK = 128
F = 4
G = 16384


def pattern(key):
    lowest = max(1, min(4 * BR, NBLK // 2 - 3))
    offsets = jax.random.permutation(jax.random.fold_in(key, 11), NBLK // 2 - lowest)[:(K - 1) // 2].astype(jnp.int32) + lowest
    indices = jnp.arange(NBLK, dtype=jnp.int32)[:, None]
    return jnp.concatenate([indices, (indices + offsets[None, :]) % NBLK, (indices - offsets[None, :]) % NBLK], axis=1).astype(jnp.int32)


def pair_codes(key):
    columns = pattern(key)
    owners = jnp.broadcast_to(jnp.arange(NBLK, dtype=jnp.int32)[:, None], columns.shape)
    lower = jnp.minimum(owners, columns)
    upper = jnp.maximum(owners, columns)
    return (columns, owners, lower, upper)


def draw_col_index(key, part):
    return pattern(key)


def draw_block_live(key, part):
    columns, owners, lower, upper = pair_codes(key)
    codes = (lower * NBLK + upper).reshape(-1)
    base_key = jax.random.fold_in(key, 23)
    hashes = jax.vmap(lambda code: jax.random.randint(jax.random.fold_in(base_key, code), (), 0, 100))(codes).reshape(lower.shape)
    region_count = NBLK // BR
    thresh = 85 + 15 * (upper // BR) // max(region_count - 1, 1)
    flags = (hashes < thresh).astype(jnp.int32)
    return jnp.where(lower == upper, 1, flags).astype(jnp.int32)


def draw_psf_blocks(key, part):
    columns, owners, lower, upper = pair_codes(key)
    codes = (lower * NBLK + upper).reshape(-1)
    above = (owners <= columns).reshape(-1)
    same = (lower == upper).reshape(-1)
    scale = 0.5 / math.sqrt(K * BS)
    base_key = jax.random.fold_in(key, 37)
    identity = jnp.eye(BS, dtype=jnp.float32)

    def one_block(freq_key, code, upper_side, on_diagonal):
        block_key = jax.random.fold_in(freq_key, code)
        raw = jnp.clip(jax.random.normal(block_key, (BS, BS), jnp.float32), -4.0, 4.0)
        flipped = jnp.where(upper_side, raw, raw.T) * scale
        centre = (raw + raw.T) * (0.70710678 * scale) * (1.0 - identity) + identity * (1.0 + 0.02 * raw)
        return jnp.where(on_diagonal, centre, flipped)

    def one_freq(index):
        freq_key = jax.random.fold_in(base_key, index)
        blocks = jax.vmap(one_block, in_axes=(None, 0, 0, 0))(freq_key, codes, above, same)
        return blocks.reshape(NBLK, K, BS, BS).astype(jnp.bfloat16)
    return lax.map(one_freq, jnp.arange(F, dtype=jnp.int32))


def steps_of(rng, extent, shards, low, high):
    def one(position, shards_of):
        draws = jax.random.uniform(jax.random.fold_in(jax.random.fold_in(rng, 6), position), (shards_of,), jnp.float32, low / len(shards), high / len(shards))
        return jnp.repeat(jnp.exp(draws), extent[position] // shards_of).reshape((-1,) + (1,) * (len(extent) - position - 1))

    level = one(*shards[0])
    for cut in shards[1:]:
        level = level * one(*cut)
    return level


def normal_values(stream_key, shape, width, most, shards=(), kind=jnp.bfloat16):
    loudness = steps_of(stream_key, shape, shards, -0.22, 0.18) if shards else 1.0
    drawn = jax.random.normal(stream_key, shape, jnp.float32) * width * loudness
    return jnp.minimum(jnp.maximum(drawn, -most), most).astype(kind)


def setup_inputs(seed: int = 0) -> dict:
    streams_of = jax.random.split(jax.random.key(seed), 5)
    return {
        "dirty_map": normal_values(streams_of[0], (F, G), 1.0, 6.0, ((0, 2), (1, 16)), jnp.float32),
        "psf_blocks": draw_psf_blocks(jax.random.fold_in(streams_of[4], 71), 0),
        "col_index": draw_col_index(jax.random.fold_in(streams_of[4], 71), 0),
        "block_live": draw_block_live(jax.random.fold_in(streams_of[4], 71), 0),
    }


def reference(dirty_map, psf_blocks, col_index, block_live):
    diagonal = jnp.diagonal(psf_blocks[:, :, 0], axis1=2, axis2=3).astype(jnp.float32).reshape(dirty_map.shape)
    alive_mask = block_live.astype(jnp.float32)
    source_map = jnp.maximum(0.0, dirty_map / diagonal)

    def apply_blocks(pair):
        blocks, values = pair
        spread = values.reshape(NBLK, BS).astype(jnp.float32)
        picked = spread[col_index] * alive_mask[:, :, None]
        applied = jnp.einsum("ikpq,ikq->ip", blocks.astype(jnp.float32), picked)
        return applied.reshape(-1)

    for iteration in range(ITERS):
        coarse = source_map.astype(jnp.bfloat16)
        applied = lax.map(apply_blocks, (psf_blocks, coarse))
        source_map = jnp.maximum(0.0, source_map + (dirty_map - applied) / diagonal)
    broadband = jnp.sum(source_map, axis=0)
    return source_map, broadband
```

```python
import functools

import jax
import jax.numpy as jnp
from jax import lax
from jax.experimental import pallas as pl
from jax.experimental.pallas import tpu as pltpu
from jax.sharding import PartitionSpec as P

ITERS = 3
MESH = pl.DeviceIdType.MESH


def partners(me, regions):
    if regions & (regions - 1):
        return [lax.rem(me + step, regions) for step in range(1, regions)]
    moves, bit = [], 1
    while bit < regions:
        moves.append(bit - 2 * bit * ((me // bit) % 2))
        bit *= 2
    masks = sorted(range(1, regions), key=lambda mask: (-(mask >> 1), mask & 1))
    return [sum((move for n, move in enumerate(moves) if mask >> n & 1), me) for mask in masks]


def kernel(
    regions,
    groups,
    dirty_hbm,
    psf_hbm,
    col_hbm,
    live_hbm,
    est_ref,
    broad_ref,
    psf,
    turned,
    dirty_ref,
    col_ref,
    live_ref,
    target_ref,
    arrived,
    pick,
    partial,
    load_sem,
    send_sem,
    recv_sem,
    broad_send,
    broad_recv,
):
    me = lax.axis_index("region")
    group = lax.axis_index("freq")
    peers = partners(me, regions)
    freq_count, row_blocks, slots, width = psf.shape[:4]
    bins = range(freq_count)

    small = [
        pltpu.make_async_copy(source, target, load_sem.at[n])
        for n, (source, target) in enumerate(
            ((dirty_hbm, dirty_ref), (live_hbm, live_ref), (col_hbm, col_ref))
        )
    ]
    first = [
        pltpu.make_async_copy(psf_hbm.at[f, :, 0], psf.at[f, :, 0], load_sem.at[3 + f]) for f in bins
    ]
    rest = pltpu.make_async_copy(
        psf_hbm.at[:, :, pl.ds(1, slots - 1)],
        psf.at[:, :, pl.ds(1, slots - 1)],
        load_sem.at[3 + freq_count],
    )
    for copy in first:
        copy.start()
    small[0].start()
    barrier = pltpu.get_barrier_semaphore()
    for peer in peers:
        pl.semaphore_signal(barrier, inc=1, device_id={"region": peer}, device_id_type=MESH)
    for step in range(1, groups):
        pl.semaphore_signal(
            barrier, inc=1, device_id={"freq": lax.rem(group + step, groups)}, device_id_type=MESH
        )
    rest.start()
    for copy in small[1:]:
        copy.start()

    row_ids = lax.broadcasted_iota(jnp.int32, (row_blocks, width), 0)
    strip = 16
    below = lax.broadcasted_iota(jnp.int32, (strip, width), 1) - lax.broadcasted_iota(
        jnp.int32, (strip, width), 0
    )

    def send(iteration, f):
        for peer in peers:
            pltpu.make_async_remote_copy(
                src_ref=arrived.at[iteration, f, me],
                dst_ref=arrived.at[iteration, f, me],
                send_sem=send_sem.at[0],
                recv_sem=recv_sem.at[iteration, f],
                device_id={"region": peer},
                device_id_type=MESH,
            ).start()

    small[0].wait()
    for f in bins:
        for i in range(row_blocks):
            target_ref[f, i : i + 1, :] = dirty_ref[f : f + 1, i * width : (i + 1) * width]

    inverse, estimates, scaled = [], [], []
    for f in bins:
        first[f].wait()
        diagonal = jnp.zeros((row_blocks, width), jnp.float32)
        for i in range(row_blocks):
            kept = jnp.zeros((strip, width), jnp.float32)
            for start in range(0, width, strip):
                piece = psf[f, i, 0, start : start + strip].astype(jnp.float32)
                kept = jnp.where(below == start, piece, kept)
            line = jnp.sum(kept, axis=0, keepdims=True)
            diagonal = jnp.where(row_ids == i, line, diagonal)
        target = target_ref[f]
        inv = 1.0 / diagonal
        estimate = jnp.maximum(0.0, target / diagonal)
        arrived[0, f, me] = estimate.astype(jnp.bfloat16)
        if f == 0:
            pl.semaphore_wait(barrier, regions - 1 + groups - 1)
        send(0, f)
        inverse.append(inv)
        scaled.append(target * inv)
        estimates.append(estimate)

    for copy in small[1:]:
        copy.wait()
    lanes = regions * row_blocks
    lane_ids = lax.broadcasted_iota(jnp.int32, (row_blocks, lanes), 1)
    for k in range(1, slots):
        wanted = jnp.where(live_ref[:, k : k + 1] > 0, col_ref[:, k : k + 1], -1)
        hit = jnp.where(lane_ids == wanted, 1.0, 0.0)
        pick[(k - 1) * row_blocks : k * row_blocks, :] = hit
    rest.wait()

    def turn(row, carry):
        f, i = row // row_blocks, row % row_blocks
        for k in range(1, slots):
            turned[f, i, (k - 1) * width : k * width, :] = psf[f, i, k].T
        return carry

    lax.fori_loop(0, freq_count * row_blocks, turn, 0)

    def sweep(iteration, estimates):
        nexts = []
        bases = []
        for f in bins:
            coarse = estimates[f].astype(jnp.bfloat16)
            near = jnp.zeros((row_blocks, width), jnp.float32)
            for i in range(row_blocks):
                product = jnp.dot(coarse, psf[f, i, 0], preferred_element_type=jnp.float32)
                near = jnp.where(row_ids == i, product, near)
            bases.append(estimates[f] + (scaled[f] - near * inverse[f]))
        for f in bins:
            others = arrived.at[iteration, f, pl.ds(0, regions - 1)]
            pltpu.make_async_copy(others, others, recv_sem.at[iteration, f]).wait()
            known = arrived[iteration, f].reshape(lanes, width)
            found = jnp.dot(pick[...].astype(jnp.bfloat16), known, preferred_element_type=jnp.float32)
            chosen = jnp.concatenate(
                [found[k * row_blocks : (k + 1) * row_blocks] for k in range(slots - 1)], axis=1
            ).astype(jnp.bfloat16)
            far = jnp.zeros((row_blocks, width), jnp.float32)
            for i in range(0, row_blocks, 2):
                blocks = jnp.concatenate([turned[f, i], turned[f, i + 1]], axis=1)
                product = jnp.dot(chosen, blocks, preferred_element_type=jnp.float32)
                for j in range(2):
                    far = jnp.where(row_ids == i + j, product[:, j * width : (j + 1) * width], far)
            estimate = jnp.maximum(0.0, bases[f] - far * inverse[f])
            nexts.append(estimate)

            @pl.when(iteration < ITERS - 1)
            def _():
                arrived[iteration + 1, f, me] = estimate.astype(jnp.bfloat16)
                send(iteration + 1, f)

        return tuple(nexts)

    estimates = lax.fori_loop(0, ITERS, sweep, tuple(estimates))
    local_sum = estimates[0]
    for f in bins[1:]:
        local_sum = local_sum + estimates[f]
    partial[group] = local_sum
    broad = []
    for step in range(1, groups):
        copy = pltpu.make_async_remote_copy(
            src_ref=partial.at[group],
            dst_ref=partial.at[group],
            send_sem=broad_send.at[step - 1],
            recv_sem=broad_recv.at[step - 1],
            device_id={"freq": lax.rem(group + step, groups)},
            device_id_type=MESH,
        )
        copy.start()
        broad.append(copy)
    for f in bins:
        for i in range(row_blocks):
            est_ref[f : f + 1, i * width : (i + 1) * width] = estimates[f][i : i + 1]
    others = arrived.at[:, :, pl.ds(0, regions - 1)]
    pltpu.make_async_copy(others, others, send_sem.at[0]).wait()
    for copy in broad:
        copy.wait()
    total = partial[0]
    for g in range(1, groups):
        total = total + partial[g]
    broad_ref[...] = total


def write_out(est_ref, broad_ref, est_out, broad_out, sems):
    copies = [
        pltpu.make_async_copy(est_ref, est_out, sems.at[0]),
        pltpu.make_async_copy(broad_ref, broad_out, sems.at[1]),
    ]
    for copy in copies:
        copy.start()
    for copy in copies:
        copy.wait()


def solution(mesh):
    regions, groups = mesh.shape["region"], mesh.shape["freq"]

    def local(dirty_map, psf_blocks, col_index, block_live):
        freq_count, row_blocks, slots, width, _ = psf_blocks.shape
        vmem = pl.BlockSpec(memory_space=pltpu.VMEM)
        anywhere = pl.BlockSpec(memory_space=pl.ANY)
        estimate, broadband = pl.pallas_call(
            functools.partial(kernel, regions, groups),
            out_shape=(
                pltpu.VMEM(dirty_map.shape, jnp.float32),
                pltpu.VMEM((row_blocks, width), jnp.float32),
            ),
            in_specs=[anywhere] * 4,
            out_specs=(vmem, vmem),
            scratch_shapes=[
                pltpu.VMEM(psf_blocks.shape, jnp.bfloat16),
                pltpu.VMEM((freq_count, row_blocks, (slots - 1) * width, width), jnp.bfloat16),
                pltpu.VMEM(dirty_map.shape, jnp.float32),
                pltpu.VMEM(col_index.shape, jnp.int32),
                pltpu.VMEM(block_live.shape, jnp.int32),
                pltpu.VMEM((freq_count, row_blocks, width), jnp.float32),
                pltpu.VMEM((ITERS, freq_count, regions, row_blocks, width), jnp.bfloat16),
                pltpu.VMEM(((slots - 1) * row_blocks, regions * row_blocks), jnp.float32),
                pltpu.VMEM((groups, row_blocks, width), jnp.float32),
                pltpu.SemaphoreType.DMA((4 + freq_count,)),
                pltpu.SemaphoreType.DMA((1,)),
                pltpu.SemaphoreType.DMA((ITERS, freq_count)),
                pltpu.SemaphoreType.DMA((max(1, groups - 1),)),
                pltpu.SemaphoreType.DMA((max(1, groups - 1),)),
            ],
            compiler_params=pltpu.CompilerParams(collective_id=0, has_side_effects=True),
        )(dirty_map, psf_blocks, col_index, block_live)
        estimate, broadband = pl.pallas_call(
            write_out,
            out_shape=(
                jax.ShapeDtypeStruct(dirty_map.shape, jnp.float32),
                jax.ShapeDtypeStruct((row_blocks, width), jnp.float32),
            ),
            in_specs=[vmem, vmem],
            out_specs=(anywhere, anywhere),
            scratch_shapes=[pltpu.SemaphoreType.DMA((2,))],
        )(
            pltpu.with_memory_space_constraint(estimate, pltpu.VMEM),
            pltpu.with_memory_space_constraint(broadband, pltpu.VMEM),
        )
        return estimate, broadband.reshape(-1)

    return jax.shard_map(
        local,
        mesh=mesh,
        in_specs=(
            P("freq", "region"),
            P("freq", "region", None, None, None),
            P("region", None),
            P("region", None),
        ),
        out_specs=(P("freq", "region"), P("region")),
        check_vma=False,
    )
```

```python
import functools

import jax
import jax.numpy as jnp
from jax import lax
from jax.experimental import pallas as pl
from jax.experimental.pallas import tpu as pltpu
from jax.sharding import PartitionSpec as P

ITERS = 3
MESH = pl.DeviceIdType.MESH


def partners(me, regions):
    if regions & (regions - 1):
        return [lax.rem(me + step, regions) for step in range(1, regions)]
    moves, bit = [], 1
    while bit < regions:
        moves.append(bit - 2 * bit * ((me // bit) % 2))
        bit *= 2
    masks = sorted(range(1, regions), key=lambda mask: (-(mask >> 1), mask & 1))
    return [sum((move for n, move in enumerate(moves) if mask >> n & 1), me) for mask in masks]


def kernel(
    regions,
    groups,
    dirty_hbm,
    psf_hbm,
    col_hbm,
    live_hbm,
    est_ref,
    broad_ref,
    psf,
    turned,
    dirty_ref,
    col_ref,
    live_ref,
    target_ref,
    arrived,
    spread,
    partial,
    load_sem,
    send_sem,
    recv_sem,
    broad_send,
    broad_recv,
):
    me = lax.axis_index("region")
    group = lax.axis_index("freq")
    peers = partners(me, regions)
    freq_count, row_blocks, slots, width = psf.shape[:4]
    bins = range(freq_count)

    maps = pltpu.make_async_copy(dirty_hbm, dirty_ref, load_sem.at[0])
    columns = pltpu.make_async_copy(col_hbm, col_ref, load_sem.at[0])
    flags = pltpu.make_async_copy(live_hbm, live_ref, load_sem.at[1])
    first = [
        pltpu.make_async_copy(psf_hbm.at[f, :, 0], psf.at[f, :, 0], load_sem.at[1 + f]) for f in bins
    ]
    rest = pltpu.make_async_copy(
        psf_hbm.at[:, :, pl.ds(1, slots - 1)],
        psf.at[:, :, pl.ds(1, slots - 1)],
        load_sem.at[1 + freq_count],
    )
    for copy in first:
        copy.start()
    maps.start()
    barrier = pltpu.get_barrier_semaphore()
    for peer in peers:
        pl.semaphore_signal(barrier, inc=1, device_id={"region": peer}, device_id_type=MESH)
    for step in range(1, groups):
        pl.semaphore_signal(
            barrier, inc=1, device_id={"freq": lax.rem(group + step, groups)}, device_id_type=MESH
        )
    rest.start()

    row_ids = lax.broadcasted_iota(jnp.int32, (row_blocks, width), 0)
    strip = 16
    below = lax.broadcasted_iota(jnp.int32, (strip, width), 1) - lax.broadcasted_iota(
        jnp.int32, (strip, width), 0
    )

    def send(iteration, f):
        for peer in peers:
            pltpu.make_async_remote_copy(
                src_ref=arrived.at[iteration, f, me],
                dst_ref=arrived.at[iteration, f, me],
                send_sem=send_sem.at[0],
                recv_sem=recv_sem.at[iteration % 2, f],
                device_id={"region": peer},
                device_id_type=MESH,
            ).start()

    maps.wait()
    columns.start()
    for f in bins:
        for i in range(row_blocks):
            target_ref[f, i : i + 1, :] = dirty_ref[f : f + 1, i * width : (i + 1) * width]

    inverse, estimates, scaled = [], [], []
    for f in bins:
        first[f].wait()
        diagonal = jnp.zeros((row_blocks, width), jnp.float32)
        for i in range(row_blocks):
            kept = jnp.zeros((strip, width), jnp.float32)
            for start in range(0, width, strip):
                piece = psf[f, i, 0, start : start + strip].astype(jnp.float32)
                kept = jnp.where(below == start, piece, kept)
            line = jnp.sum(kept, axis=0, keepdims=True)
            diagonal = jnp.where(row_ids == i, line, diagonal)
        target = target_ref[f]
        inv = 1.0 / diagonal
        estimate = jnp.maximum(0.0, target / diagonal)
        arrived[0, f, me] = estimate.astype(jnp.bfloat16)
        if f == 0:
            pl.semaphore_wait(barrier, regions - 1 + groups - 1)
        send(0, f)
        if f == 0:
            flags.start()
        inverse.append(inv)
        scaled.append(target * inv)
        estimates.append(estimate)

    columns.wait()
    flags.wait()
    blocks_all = regions * row_blocks
    starts = [col_ref[0, k] for k in range(1, slots)]
    alive = [
        jnp.broadcast_to(live_ref[:, k : k + 1].astype(jnp.float32), (row_blocks, width))
        for k in range(1, slots)
    ]
    rest.wait()

    def turn(row, carry):
        f, i = row // row_blocks, row % row_blocks
        for k in range(1, slots):
            turned[f, i, (k - 1) * width : k * width, :] = psf[f, i, k].T
        return carry

    lax.fori_loop(0, freq_count * row_blocks, turn, 0)

    def sweep(iteration, estimates):
        nexts = []
        bases = []
        for f in bins:
            coarse = estimates[f].astype(jnp.bfloat16)
            near = jnp.zeros((row_blocks, width), jnp.float32)
            for i in range(row_blocks):
                product = jnp.dot(coarse, psf[f, i, 0], preferred_element_type=jnp.float32)
                near = jnp.where(row_ids == i, product, near)
            bases.append(estimates[f] + (scaled[f] - near * inverse[f]))
        for f in bins:
            others = arrived.at[iteration, f, pl.ds(0, regions - 1)]
            pltpu.make_async_copy(others, others, recv_sem.at[iteration % 2, f]).wait()
            known = arrived[iteration, f].astype(jnp.float32).reshape(blocks_all, width)
            spread[f, :blocks_all] = known
            spread[f, blocks_all:] = known[:row_blocks]
            found = [spread[f, pl.ds(starts[k], row_blocks)] * alive[k] for k in range(slots - 1)]
            chosen = jnp.concatenate(found, axis=1).astype(jnp.bfloat16)
            far = jnp.zeros((row_blocks, width), jnp.float32)
            for i in range(0, row_blocks, 2):
                blocks = jnp.concatenate([turned[f, i], turned[f, i + 1]], axis=1)
                product = jnp.dot(chosen, blocks, preferred_element_type=jnp.float32)
                for j in range(2):
                    far = jnp.where(row_ids == i + j, product[:, j * width : (j + 1) * width], far)
            estimate = jnp.maximum(0.0, bases[f] - far * inverse[f])
            nexts.append(estimate)

            @pl.when(iteration < ITERS - 1)
            def _():
                arrived[iteration + 1, f, me] = estimate.astype(jnp.bfloat16)
                send(iteration + 1, f)

        return tuple(nexts)

    estimates = lax.fori_loop(0, ITERS, sweep, tuple(estimates))
    local_sum = estimates[0]
    for f in bins[1:]:
        local_sum = local_sum + estimates[f]
    partial[group] = local_sum
    broad = []
    for step in range(1, groups):
        copy = pltpu.make_async_remote_copy(
            src_ref=partial.at[group],
            dst_ref=partial.at[group],
            send_sem=broad_send.at[step - 1],
            recv_sem=broad_recv.at[step - 1],
            device_id={"freq": lax.rem(group + step, groups)},
            device_id_type=MESH,
        )
        copy.start()
        broad.append(copy)
    for f in bins:
        for i in range(row_blocks):
            est_ref[f : f + 1, i * width : (i + 1) * width] = estimates[f][i : i + 1]
    others = arrived.at[:, :, pl.ds(0, regions - 1)]
    pltpu.make_async_copy(others, others, send_sem.at[0]).wait()
    for copy in broad:
        copy.wait()
    total = partial[0]
    for g in range(1, groups):
        total = total + partial[g]
    broad_ref[...] = total


def write_out(est_ref, broad_ref, est_out, broad_out, sems):
    copies = [
        pltpu.make_async_copy(est_ref, est_out, sems.at[0]),
        pltpu.make_async_copy(broad_ref, broad_out, sems.at[1]),
    ]
    for copy in copies:
        copy.start()
    for copy in copies:
        copy.wait()


def solution(mesh):
    regions, groups = mesh.shape["region"], mesh.shape["freq"]

    def local(dirty_map, psf_blocks, col_index, block_live):
        freq_count, row_blocks, slots, width, _ = psf_blocks.shape
        vmem = pl.BlockSpec(memory_space=pltpu.VMEM)
        anywhere = pl.BlockSpec(memory_space=pl.ANY)
        estimate, broadband = pl.pallas_call(
            functools.partial(kernel, regions, groups),
            out_shape=(
                pltpu.VMEM(dirty_map.shape, jnp.float32),
                pltpu.VMEM((row_blocks, width), jnp.float32),
            ),
            in_specs=[anywhere] * 4,
            out_specs=(vmem, vmem),
            scratch_shapes=[
                pltpu.VMEM(psf_blocks.shape, jnp.bfloat16),
                pltpu.VMEM((freq_count, row_blocks, (slots - 1) * width, width), jnp.bfloat16),
                pltpu.VMEM(dirty_map.shape, jnp.float32),
                pltpu.SMEM(col_index.shape, jnp.int32),
                pltpu.VMEM(block_live.shape, jnp.int32),
                pltpu.VMEM((freq_count, row_blocks, width), jnp.float32),
                pltpu.VMEM((ITERS, freq_count, regions, row_blocks, width), jnp.bfloat16),
                pltpu.VMEM((freq_count, (regions + 1) * row_blocks, width), jnp.float32),
                pltpu.VMEM((groups, row_blocks, width), jnp.float32),
                pltpu.SemaphoreType.DMA((2 + freq_count,)),
                pltpu.SemaphoreType.DMA((1,)),
                pltpu.SemaphoreType.DMA((2, freq_count)),
                pltpu.SemaphoreType.DMA((max(1, groups - 1),)),
                pltpu.SemaphoreType.DMA((max(1, groups - 1),)),
            ],
            compiler_params=pltpu.CompilerParams(collective_id=0, has_side_effects=True),
        )(dirty_map, psf_blocks, col_index, block_live)
        estimate, broadband = pl.pallas_call(
            write_out,
            out_shape=(
                jax.ShapeDtypeStruct(dirty_map.shape, jnp.float32),
                jax.ShapeDtypeStruct((row_blocks, width), jnp.float32),
            ),
            in_specs=[vmem, vmem],
            out_specs=(anywhere, anywhere),
            scratch_shapes=[pltpu.SemaphoreType.DMA((2,))],
        )(
            pltpu.with_memory_space_constraint(estimate, pltpu.VMEM),
            pltpu.with_memory_space_constraint(broadband, pltpu.VMEM),
        )
        return estimate, broadband.reshape(-1)

    return jax.shard_map(
        local,
        mesh=mesh,
        in_specs=(
            P("freq", "region"),
            P("freq", "region", None, None, None),
            P("region", None),
            P("region", None),
        ),
        out_specs=(P("freq", "region"), P("region")),
        check_vma=False,
    )
```

```python
import functools

import jax
import jax.numpy as jnp
from jax import lax
from jax.experimental import pallas as pl
from jax.experimental.pallas import tpu as pltpu
from jax.sharding import PartitionSpec as P

ITERS = 3
GAP = 2
MESH = pl.DeviceIdType.MESH


def partners(me, regions):
    if regions & (regions - 1):
        return [lax.rem(me + step, regions) for step in range(1, regions)]
    moves, bit = [], 1
    while bit < regions:
        moves.append(bit - 2 * bit * ((me // bit) % 2))
        bit *= 2
    masks = sorted(range(1, regions), key=lambda mask: (-(mask >> 1), mask & 1))
    return [sum((move for n, move in enumerate(moves) if mask >> n & 1), me) for mask in masks]


def kernel(
    regions,
    groups,
    dirty_hbm,
    psf_hbm,
    col_hbm,
    live_hbm,
    est_ref,
    broad_ref,
    psf,
    turned,
    dirty_ref,
    col_ref,
    live_ref,
    target_ref,
    arrived,
    spread,
    partial,
    load_sem,
    send_sem,
    recv_sem,
    broad_send,
    broad_recv,
):
    me = lax.axis_index("region")
    group = lax.axis_index("freq")
    peers = partners(me, regions)
    freq_count, row_blocks, slots, width = psf.shape[:4]
    bins = range(freq_count)

    maps = pltpu.make_async_copy(dirty_hbm, dirty_ref, load_sem.at[0])
    columns = pltpu.make_async_copy(col_hbm, col_ref, load_sem.at[0])
    flags = pltpu.make_async_copy(live_hbm, live_ref, load_sem.at[1])
    first = [
        pltpu.make_async_copy(psf_hbm.at[f, :, 0], psf.at[f, :, 0], load_sem.at[1 + f]) for f in bins
    ]
    rest = pltpu.make_async_copy(
        psf_hbm.at[:, :, pl.ds(1, slots - 1)],
        psf.at[:, :, pl.ds(1, slots - 1)],
        load_sem.at[1 + freq_count],
    )
    for copy in first:
        copy.start()
    maps.start()
    barrier = pltpu.get_barrier_semaphore()
    for peer in peers:
        pl.semaphore_signal(barrier, inc=1, device_id={"region": peer}, device_id_type=MESH)
    for step in range(1, groups):
        pl.semaphore_signal(
            barrier, inc=1, device_id={"freq": lax.rem(group + step, groups)}, device_id_type=MESH
        )
    rest.start()

    row_ids = lax.broadcasted_iota(jnp.int32, (row_blocks, width), 0)
    strip = 16
    below = lax.broadcasted_iota(jnp.int32, (strip, width), 1) - lax.broadcasted_iota(
        jnp.int32, (strip, width), 0
    )

    def send(iteration, f, between=()):
        between = list(between)
        for n, peer in enumerate(peers):
            pltpu.make_async_remote_copy(
                src_ref=arrived.at[iteration, f, me],
                dst_ref=arrived.at[iteration, f, me],
                send_sem=send_sem.at[0],
                recv_sem=recv_sem.at[iteration % 2, f],
                device_id={"region": peer},
                device_id_type=MESH,
            ).start()
            if between and n % GAP == GAP - 1:
                between.pop(0)()
        for part in between:
            part()

    maps.wait()
    columns.start()
    for f in bins:
        for i in range(row_blocks):
            target_ref[f, i : i + 1, :] = dirty_ref[f : f + 1, i * width : (i + 1) * width]

    inverse, estimates, scaled = [], [], []
    for f in bins:
        first[f].wait()
        diagonal = jnp.zeros((row_blocks, width), jnp.float32)
        for i in range(row_blocks):
            kept = jnp.zeros((strip, width), jnp.float32)
            for start in range(0, width, strip):
                piece = psf[f, i, 0, start : start + strip].astype(jnp.float32)
                kept = jnp.where(below == start, piece, kept)
            line = jnp.sum(kept, axis=0, keepdims=True)
            diagonal = jnp.where(row_ids == i, line, diagonal)
        target = target_ref[f]
        inv = 1.0 / diagonal
        estimate = jnp.maximum(0.0, target / diagonal)
        arrived[0, f, me] = estimate.astype(jnp.bfloat16)
        if f == 0:
            pl.semaphore_wait(barrier, regions - 1 + groups - 1)
        send(0, f)
        if f == 0:
            flags.start()
        inverse.append(inv)
        scaled.append(target * inv)
        estimates.append(estimate)

    columns.wait()
    flags.wait()
    blocks_all = regions * row_blocks
    starts = [col_ref[0, k] for k in range(1, slots)]
    alive = [
        jnp.broadcast_to(live_ref[:, k : k + 1].astype(jnp.float32), (row_blocks, width))
        for k in range(1, slots)
    ]
    rest.wait()

    pairs = row_blocks // 2
    depths = (slots - 1) // 2

    def turn(row, carry):
        f, q = row // pairs, row % pairs
        for j in range(2):
            for k in range(slots - 1):
                rows = slice(k % 2 * width, k % 2 * width + width)
                turned[f, q, k // 2, rows, j * width : (j + 1) * width] = psf[f, 2 * q + j, 1 + k].T
        return carry

    lax.fori_loop(0, freq_count * pairs, turn, 0)

    def near(accs, f, estimate):
        coarse = jnp.concatenate([estimate, jnp.zeros_like(estimate)], axis=0)
        coarse = jnp.concatenate([coarse, jnp.zeros_like(coarse)], axis=1).astype(jnp.bfloat16)
        for h in range(2):
            for m in range(2):
                i = 2 * (2 * m + h)
                side = [jnp.concatenate([psf[f, i + j, 0], psf[f, i + j, 1]], axis=0) for j in range(2)]
                pltpu.matmul_push_rhs(jnp.concatenate(side, axis=1), h, m)
        for h in range(2):
            for m in range(2):
                pltpu.matmul_acc_lhs(accs[f][m][h], coarse, h)

    nothing = jnp.zeros((2 * row_blocks, 2 * width), jnp.bfloat16)

    def ready(accs, f):
        def part(n, m):
            pltpu.matmul_push_rhs(turned[f, 2 * m, n], n // 2, m)
            if n == 0:
                pltpu.matmul_acc_lhs(accs[f][m][0], nothing, 0)

        return [functools.partial(part, n, m) for n in range(3) for m in range(2)]

    def multiply(accs, f, iteration):
        others = arrived.at[iteration, f, pl.ds(0, regions - 1)]
        pltpu.make_async_copy(others, others, recv_sem.at[iteration % 2, f]).wait()
        known = arrived[iteration, f].astype(jnp.float32).reshape(blocks_all, width)
        spread[f, :blocks_all] = known
        spread[f, blocks_all:] = known[:row_blocks]
        found = [spread[f, pl.ds(starts[k], row_blocks)] * alive[k] for k in range(slots - 1)]
        pad = jnp.zeros((row_blocks, 2 * width), jnp.float32)
        left = [
            jnp.concatenate([jnp.concatenate(found[2 * d : 2 * d + 2], axis=1), pad], axis=0).astype(jnp.bfloat16)
            for d in range(depths)
        ]
        for m in range(2):
            pltpu.matmul_acc_lhs(accs[f][m][0], left[0])
        for m in range(2):
            pltpu.matmul_acc_lhs(accs[f][m][0], left[1], 0)
            pltpu.matmul_push_rhs(turned[f, 2 * m + 1, 0], 0, m)
        for m in range(2):
            pltpu.matmul_acc_lhs(accs[f][m][0], left[2], 1)
            pltpu.matmul_push_rhs(turned[f, 2 * m + 1, 1], 1, m)
        for m in range(2):
            pltpu.matmul_acc_lhs(accs[f][m][1], left[0], 0)
            pltpu.matmul_push_rhs(turned[f, 2 * m + 1, 2], 0, m)
        for m in range(2):
            pltpu.matmul_acc_lhs(accs[f][m][1], left[1], 1)
        for m in range(2):
            pltpu.matmul_acc_lhs(accs[f][m][1], left[2], 0)
        applied = jnp.zeros((row_blocks, width), jnp.float32)
        for m in range(2):
            for h in range(2):
                product = pltpu.matmul_pop(accs[f][m][h])[:row_blocks]
                for j in range(2):
                    part = product[:, j * width : (j + 1) * width]
                    applied = jnp.where(row_ids == 2 * (2 * m + h) + j, part, applied)
        return applied

    shape = (2 * row_blocks, 2 * width)

    def sweep(iteration, estimates, last):
        def body(*refs):
            refs = list(refs)
            accs = [[[refs.pop(0) for h in range(2)] for m in range(2)] for f in bins]
            for f in bins:
                near(accs, f, estimates[f])
            nexts = []
            for part in ready(accs, 0):
                part()
            for f in bins:
                applied = multiply(accs, f, iteration)
                estimate = jnp.maximum(0.0, (estimates[f] + scaled[f]) - applied * inverse[f])
                nexts.append(estimate)
                coming = ready(accs, f + 1) if f + 1 < freq_count else []
                if last:
                    for part in coming:
                        part()
                else:
                    arrived[iteration + 1, f, me] = estimate.astype(jnp.bfloat16)
                    send(iteration + 1, f, coming)
            return tuple(nexts)

        return pl.run_scoped(
            body, *[pltpu.ACC(m)(shape, jnp.float32) for f in bins for m in range(2) for h in range(2)]
        )

    estimates = lax.fori_loop(0, ITERS - 1, functools.partial(sweep, last=False), tuple(estimates))
    estimates = sweep(ITERS - 1, estimates, last=True)
    local_sum = estimates[0]
    for f in bins[1:]:
        local_sum = local_sum + estimates[f]
    partial[group] = local_sum
    broad = []
    for step in range(1, groups):
        copy = pltpu.make_async_remote_copy(
            src_ref=partial.at[group],
            dst_ref=partial.at[group],
            send_sem=broad_send.at[step - 1],
            recv_sem=broad_recv.at[step - 1],
            device_id={"freq": lax.rem(group + step, groups)},
            device_id_type=MESH,
        )
        copy.start()
        broad.append(copy)
    for f in bins:
        for i in range(row_blocks):
            est_ref[f : f + 1, i * width : (i + 1) * width] = estimates[f][i : i + 1]
    others = arrived.at[:, :, pl.ds(0, regions - 1)]
    pltpu.make_async_copy(others, others, send_sem.at[0]).wait()
    for copy in broad:
        copy.wait()
    total = partial[0]
    for g in range(1, groups):
        total = total + partial[g]
    broad_ref[...] = total


def write_out(est_ref, broad_ref, est_out, broad_out, sems):
    copies = [
        pltpu.make_async_copy(est_ref, est_out, sems.at[0]),
        pltpu.make_async_copy(broad_ref, broad_out, sems.at[1]),
    ]
    for copy in copies:
        copy.start()
    for copy in copies:
        copy.wait()


def solution(mesh):
    regions, groups = mesh.shape["region"], mesh.shape["freq"]

    def local(dirty_map, psf_blocks, col_index, block_live):
        freq_count, row_blocks, slots, width, _ = psf_blocks.shape
        vmem = pl.BlockSpec(memory_space=pltpu.VMEM)
        anywhere = pl.BlockSpec(memory_space=pl.ANY)
        estimate, broadband = pl.pallas_call(
            functools.partial(kernel, regions, groups),
            out_shape=(
                pltpu.VMEM(dirty_map.shape, jnp.float32),
                pltpu.VMEM((row_blocks, width), jnp.float32),
            ),
            in_specs=[anywhere] * 4,
            out_specs=(vmem, vmem),
            scratch_shapes=[
                pltpu.VMEM(psf_blocks.shape, jnp.bfloat16),
                pltpu.VMEM((freq_count, row_blocks // 2, (slots - 1) // 2, 2 * width, 2 * width), jnp.bfloat16),
                pltpu.VMEM(dirty_map.shape, jnp.float32),
                pltpu.SMEM(col_index.shape, jnp.int32),
                pltpu.VMEM(block_live.shape, jnp.int32),
                pltpu.VMEM((freq_count, row_blocks, width), jnp.float32),
                pltpu.VMEM((ITERS, freq_count, regions, row_blocks, width), jnp.bfloat16),
                pltpu.VMEM((freq_count, (regions + 1) * row_blocks, width), jnp.float32),
                pltpu.VMEM((groups, row_blocks, width), jnp.float32),
                pltpu.SemaphoreType.DMA((2 + freq_count,)),
                pltpu.SemaphoreType.DMA((1,)),
                pltpu.SemaphoreType.DMA((2, freq_count)),
                pltpu.SemaphoreType.DMA((max(1, groups - 1),)),
                pltpu.SemaphoreType.DMA((max(1, groups - 1),)),
            ],
            compiler_params=pltpu.CompilerParams(collective_id=0, has_side_effects=True),
        )(dirty_map, psf_blocks, col_index, block_live)
        estimate, broadband = pl.pallas_call(
            write_out,
            out_shape=(
                jax.ShapeDtypeStruct(dirty_map.shape, jnp.float32),
                jax.ShapeDtypeStruct((row_blocks, width), jnp.float32),
            ),
            in_specs=[vmem, vmem],
            out_specs=(anywhere, anywhere),
            scratch_shapes=[pltpu.SemaphoreType.DMA((2,))],
        )(
            pltpu.with_memory_space_constraint(estimate, pltpu.VMEM),
            pltpu.with_memory_space_constraint(broadband, pltpu.VMEM),
        )
        return estimate, broadband.reshape(-1)

    return jax.shard_map(
        local,
        mesh=mesh,
        in_specs=(
            P("freq", "region"),
            P("freq", "region", None, None, None),
            P("region", None),
            P("region", None),
        ),
        out_specs=(P("freq", "region"), P("region")),
        check_vma=False,
    )
```

```python
import functools

import jax
import jax.numpy as jnp
from jax import lax
from jax.experimental import pallas as pl
from jax.experimental.pallas import tpu as pltpu
from jax.sharding import PartitionSpec as P

ITERS = 3
GAP = 2
MESH = pl.DeviceIdType.MESH


def partners(me, regions):
    if regions & (regions - 1):
        return [lax.rem(me + step, regions) for step in range(1, regions)]
    moves, bit = [], 1
    while bit < regions:
        moves.append(bit - 2 * bit * ((me // bit) % 2))
        bit *= 2
    masks = sorted(range(1, regions), key=lambda mask: (mask & 1, -mask))
    return [sum((move for n, move in enumerate(moves) if mask >> n & 1), me) for mask in masks]


def kernel(
    regions,
    groups,
    dirty_hbm,
    psf_hbm,
    col_hbm,
    live_hbm,
    est_ref,
    broad_ref,
    psf,
    turned,
    dirty_ref,
    col_ref,
    live_ref,
    target_ref,
    arrived,
    spread,
    partial,
    load_sem,
    send_sem,
    recv_sem,
    broad_send,
    broad_recv,
):
    me = lax.axis_index("region")
    group = lax.axis_index("freq")
    peers = partners(me, regions)
    freq_count, row_blocks, slots, width = psf.shape[:4]
    bins = range(freq_count)

    maps = pltpu.make_async_copy(dirty_hbm, dirty_ref, load_sem.at[0])
    columns = pltpu.make_async_copy(col_hbm, col_ref, load_sem.at[0])
    flags = pltpu.make_async_copy(live_hbm, live_ref, load_sem.at[1])
    first = [
        pltpu.make_async_copy(psf_hbm.at[f, :, 0], psf.at[f, :, 0], load_sem.at[1 + f]) for f in bins
    ]
    rest = pltpu.make_async_copy(
        psf_hbm.at[:, :, pl.ds(1, slots - 1)],
        psf.at[:, :, pl.ds(1, slots - 1)],
        load_sem.at[1 + freq_count],
    )
    barrier = pltpu.get_barrier_semaphore()
    for peer in peers:
        pl.semaphore_signal(barrier, inc=1, device_id={"region": peer}, device_id_type=MESH)
    for step in range(1, groups):
        pl.semaphore_signal(
            barrier, inc=1, device_id={"freq": lax.rem(group + step, groups)}, device_id_type=MESH
        )
    for copy in first:
        copy.start()
    maps.start()
    rest.start()

    row_ids = lax.broadcasted_iota(jnp.int32, (row_blocks, width), 0)
    strip = 16
    below = lax.broadcasted_iota(jnp.int32, (strip, width), 1) - lax.broadcasted_iota(
        jnp.int32, (strip, width), 0
    )

    def send(iteration, f, between=()):
        between = list(between)
        for n, peer in enumerate(peers):
            pltpu.make_async_remote_copy(
                src_ref=arrived.at[iteration, f, me],
                dst_ref=arrived.at[iteration, f, me],
                send_sem=send_sem.at[0],
                recv_sem=recv_sem.at[iteration % 2, f],
                device_id={"region": peer},
                device_id_type=MESH,
            ).start()
            if between and n % GAP == GAP - 1:
                between.pop(0)()
        for part in between:
            part()

    maps.wait()
    columns.start()
    for f in bins:
        for i in range(row_blocks):
            target_ref[f, i : i + 1, :] = dirty_ref[f : f + 1, i * width : (i + 1) * width]

    for copy in first:
        copy.wait()
    flags.start()
    inverse, estimates, scaled = [], [], []
    for f in bins:
        diagonal = jnp.zeros((row_blocks, width), jnp.float32)
        for i in range(row_blocks):
            kept = jnp.zeros((strip, width), jnp.float32)
            for start in range(0, width, strip):
                piece = psf[f, i, 0, start : start + strip].astype(jnp.float32)
                kept = jnp.where(below == start, piece, kept)
            line = jnp.sum(kept, axis=0, keepdims=True)
            diagonal = jnp.where(row_ids == i, line, diagonal)
        target = target_ref[f]
        inv = 1.0 / diagonal
        estimate = jnp.maximum(0.0, target / diagonal)
        arrived[0, f, me] = estimate.astype(jnp.bfloat16)
        inverse.append(inv)
        scaled.append(target * inv)
        estimates.append(estimate)

    pl.semaphore_wait(barrier, regions - 1 + groups - 1)
    for f in bins:
        send(0, f)
    columns.wait()
    flags.wait()
    blocks_all = regions * row_blocks
    starts = [col_ref[0, k] for k in range(1, slots)]
    alive = [
        jnp.broadcast_to(live_ref[:, k : k + 1].astype(jnp.float32), (row_blocks, width))
        for k in range(1, slots)
    ]
    rest.wait()

    pairs = row_blocks // 2
    depths = (slots - 1) // 2

    def turn(row, carry):
        f, q = row // pairs, row % pairs
        for j in range(2):
            for k in range(slots - 1):
                rows = slice(k % 2 * width, k % 2 * width + width)
                turned[f, q, k // 2, rows, j * width : (j + 1) * width] = psf[f, 2 * q + j, 1 + k].T
        return carry

    lax.fori_loop(0, freq_count * pairs, turn, 0)

    def near(accs, f, estimate):
        coarse = jnp.concatenate([estimate, jnp.zeros_like(estimate)], axis=0)
        coarse = jnp.concatenate([coarse, jnp.zeros_like(coarse)], axis=1).astype(jnp.bfloat16)
        for h in range(2):
            for m in range(2):
                i = 2 * (2 * m + h)
                side = [jnp.concatenate([psf[f, i + j, 0], psf[f, i + j, 1]], axis=0) for j in range(2)]
                pltpu.matmul_push_rhs(jnp.concatenate(side, axis=1), h, m)
        for h in range(2):
            for m in range(2):
                pltpu.matmul_acc_lhs(accs[f][m][h], coarse, h)

    nothing = jnp.zeros((2 * row_blocks, 2 * width), jnp.bfloat16)

    def ready(accs, f):
        def part(n, m):
            pltpu.matmul_push_rhs(turned[f, 2 * m, n], n // 2, m)
            if n == 0:
                pltpu.matmul_acc_lhs(accs[f][m][0], nothing, 0)

        return [functools.partial(part, n, m) for n in range(3) for m in range(2)]

    def multiply(accs, f, iteration):
        others = arrived.at[iteration, f, pl.ds(0, regions - 1)]
        pltpu.make_async_copy(others, others, recv_sem.at[iteration % 2, f]).wait()
        known = arrived[iteration, f].astype(jnp.float32).reshape(blocks_all, width)
        spread[f, :blocks_all] = known
        spread[f, blocks_all:] = known[:row_blocks]
        found = [spread[f, pl.ds(starts[k], row_blocks)] * alive[k] for k in range(slots - 1)]
        pad = jnp.zeros((row_blocks, 2 * width), jnp.float32)
        left = [
            jnp.concatenate([jnp.concatenate(found[2 * d : 2 * d + 2], axis=1), pad], axis=0).astype(jnp.bfloat16)
            for d in range(depths)
        ]
        for m in range(2):
            pltpu.matmul_acc_lhs(accs[f][m][0], left[0])
        for m in range(2):
            pltpu.matmul_acc_lhs(accs[f][m][0], left[1], 0)
            pltpu.matmul_push_rhs(turned[f, 2 * m + 1, 0], 0, m)
        for m in range(2):
            pltpu.matmul_acc_lhs(accs[f][m][0], left[2], 1)
            pltpu.matmul_push_rhs(turned[f, 2 * m + 1, 1], 1, m)
        for m in range(2):
            pltpu.matmul_acc_lhs(accs[f][m][1], left[0], 0)
            pltpu.matmul_push_rhs(turned[f, 2 * m + 1, 2], 0, m)
        for m in range(2):
            pltpu.matmul_acc_lhs(accs[f][m][1], left[1], 1)
        for m in range(2):
            pltpu.matmul_acc_lhs(accs[f][m][1], left[2], 0)
        applied = jnp.zeros((row_blocks, width), jnp.float32)
        for m in range(2):
            for h in range(2):
                product = pltpu.matmul_pop(accs[f][m][h])[:row_blocks]
                for j in range(2):
                    part = product[:, j * width : (j + 1) * width]
                    applied = jnp.where(row_ids == 2 * (2 * m + h) + j, part, applied)
        return applied

    shape = (2 * row_blocks, 2 * width)

    def sweep(iteration, estimates, last):
        def body(*refs):
            refs = list(refs)
            accs = [[[refs.pop(0) for h in range(2)] for m in range(2)] for f in bins]
            for f in bins:
                near(accs, f, estimates[f])
            nexts = []
            for part in ready(accs, 0):
                part()
            for f in bins:
                applied = multiply(accs, f, iteration)
                estimate = jnp.maximum(0.0, (estimates[f] + scaled[f]) - applied * inverse[f])
                nexts.append(estimate)
                coming = ready(accs, f + 1) if f + 1 < freq_count else []
                if last:
                    for part in coming:
                        part()
                else:
                    arrived[iteration + 1, f, me] = estimate.astype(jnp.bfloat16)
                    send(iteration + 1, f, coming)
            return tuple(nexts)

        return pl.run_scoped(
            body, *[pltpu.ACC(m)(shape, jnp.float32) for f in bins for m in range(2) for h in range(2)]
        )

    estimates = lax.fori_loop(0, ITERS - 1, functools.partial(sweep, last=False), tuple(estimates))
    estimates = sweep(ITERS - 1, estimates, last=True)
    local_sum = estimates[0]
    for f in bins[1:]:
        local_sum = local_sum + estimates[f]
    partial[group] = local_sum
    broad = []
    for step in range(1, groups):
        copy = pltpu.make_async_remote_copy(
            src_ref=partial.at[group],
            dst_ref=partial.at[group],
            send_sem=broad_send.at[step - 1],
            recv_sem=broad_recv.at[step - 1],
            device_id={"freq": lax.rem(group + step, groups)},
            device_id_type=MESH,
        )
        copy.start()
        broad.append(copy)
    for f in bins:
        for i in range(row_blocks):
            est_ref[f : f + 1, i * width : (i + 1) * width] = estimates[f][i : i + 1]
    others = arrived.at[:, :, pl.ds(0, regions - 1)]
    pltpu.make_async_copy(others, others, send_sem.at[0]).wait()
    for copy in broad:
        copy.wait()
    total = partial[0]
    for g in range(1, groups):
        total = total + partial[g]
    broad_ref[...] = total


def write_out(est_ref, broad_ref, est_out, broad_out, sems):
    copies = [
        pltpu.make_async_copy(est_ref, est_out, sems.at[0]),
        pltpu.make_async_copy(broad_ref, broad_out, sems.at[1]),
    ]
    for copy in copies:
        copy.start()
    for copy in copies:
        copy.wait()


def solution(mesh):
    regions, groups = mesh.shape["region"], mesh.shape["freq"]

    def local(dirty_map, psf_blocks, col_index, block_live):
        freq_count, row_blocks, slots, width, _ = psf_blocks.shape
        vmem = pl.BlockSpec(memory_space=pltpu.VMEM)
        anywhere = pl.BlockSpec(memory_space=pl.ANY)
        estimate, broadband = pl.pallas_call(
            functools.partial(kernel, regions, groups),
            out_shape=(
                pltpu.VMEM(dirty_map.shape, jnp.float32),
                pltpu.VMEM((row_blocks, width), jnp.float32),
            ),
            in_specs=[anywhere] * 4,
            out_specs=(vmem, vmem),
            scratch_shapes=[
                pltpu.VMEM(psf_blocks.shape, jnp.bfloat16),
                pltpu.VMEM((freq_count, row_blocks // 2, (slots - 1) // 2, 2 * width, 2 * width), jnp.bfloat16),
                pltpu.VMEM(dirty_map.shape, jnp.float32),
                pltpu.SMEM(col_index.shape, jnp.int32),
                pltpu.VMEM(block_live.shape, jnp.int32),
                pltpu.VMEM((freq_count, row_blocks, width), jnp.float32),
                pltpu.VMEM((ITERS, freq_count, regions, row_blocks, width), jnp.bfloat16),
                pltpu.VMEM((freq_count, (regions + 1) * row_blocks, width), jnp.float32),
                pltpu.VMEM((groups, row_blocks, width), jnp.float32),
                pltpu.SemaphoreType.DMA((2 + freq_count,)),
                pltpu.SemaphoreType.DMA((1,)),
                pltpu.SemaphoreType.DMA((2, freq_count)),
                pltpu.SemaphoreType.DMA((max(1, groups - 1),)),
                pltpu.SemaphoreType.DMA((max(1, groups - 1),)),
            ],
            compiler_params=pltpu.CompilerParams(collective_id=0, has_side_effects=True),
        )(dirty_map, psf_blocks, col_index, block_live)
        estimate, broadband = pl.pallas_call(
            write_out,
            out_shape=(
                jax.ShapeDtypeStruct(dirty_map.shape, jnp.float32),
                jax.ShapeDtypeStruct((row_blocks, width), jnp.float32),
            ),
            in_specs=[vmem, vmem],
            out_specs=(anywhere, anywhere),
            scratch_shapes=[pltpu.SemaphoreType.DMA((2,))],
        )(
            pltpu.with_memory_space_constraint(estimate, pltpu.VMEM),
            pltpu.with_memory_space_constraint(broadband, pltpu.VMEM),
        )
        return estimate, broadband.reshape(-1)

    return jax.shard_map(
        local,
        mesh=mesh,
        in_specs=(
            P("freq", "region"),
            P("freq", "region", None, None, None),
            P("region", None),
            P("region", None),
        ),
        out_specs=(P("freq", "region"), P("region")),
        check_vma=False,
    )
```

```python
import functools

import jax
import jax.numpy as jnp
from jax import lax
from jax.experimental import pallas as pl
from jax.experimental.pallas import tpu as pltpu
from jax.sharding import PartitionSpec as P

ITERS = 3
GAP = 2
MESH = pl.DeviceIdType.MESH


def partners(me, regions):
    if regions & (regions - 1):
        return [lax.rem(me + step, regions) for step in range(1, regions)]
    moves, bit = [], 1
    while bit < regions:
        moves.append(bit - 2 * bit * ((me // bit) % 2))
        bit *= 2
    masks = sorted(range(1, regions), key=lambda mask: (mask & 1, -mask))
    return [sum((move for n, move in enumerate(moves) if mask >> n & 1), me) for mask in masks]


def kernel(
    regions,
    groups,
    dirty_hbm,
    psf_hbm,
    col_hbm,
    live_hbm,
    est_ref,
    broad_ref,
    psf,
    turned,
    dirty_ref,
    col_ref,
    live_ref,
    target_ref,
    arrived,
    spread,
    partial,
    load_sem,
    send_sem,
    recv_sem,
    broad_send,
    broad_recv,
):
    me = lax.axis_index("region")
    group = lax.axis_index("freq")
    peers = partners(me, regions)
    freq_count, row_blocks, slots, width = psf.shape[:4]
    bins = range(freq_count)

    maps = pltpu.make_async_copy(dirty_hbm, dirty_ref, load_sem.at[0])
    columns = pltpu.make_async_copy(col_hbm, col_ref, load_sem.at[0])
    flags = pltpu.make_async_copy(live_hbm, live_ref, load_sem.at[1])
    first = [
        pltpu.make_async_copy(psf_hbm.at[f, :, 0], psf.at[f, :, 0], load_sem.at[1 + f]) for f in bins
    ]
    rest = pltpu.make_async_copy(
        psf_hbm.at[:, :, pl.ds(1, slots - 1)],
        psf.at[:, :, pl.ds(1, slots - 1)],
        load_sem.at[1 + freq_count],
    )
    barrier = pltpu.get_barrier_semaphore()
    for peer in peers:
        pl.semaphore_signal(barrier, inc=1, device_id={"region": peer}, device_id_type=MESH)
    for step in range(1, groups):
        pl.semaphore_signal(
            barrier, inc=1, device_id={"freq": lax.rem(group + step, groups)}, device_id_type=MESH
        )
    for copy in first:
        copy.start()
    maps.start()
    rest.start()

    row_ids = lax.broadcasted_iota(jnp.int32, (row_blocks, width), 0)
    strip = 16
    below = lax.broadcasted_iota(jnp.int32, (strip, width), 1) - lax.broadcasted_iota(
        jnp.int32, (strip, width), 0
    )

    def send(iteration, f, between=()):
        between = list(between)
        for n, peer in enumerate(peers):
            pltpu.make_async_remote_copy(
                src_ref=arrived.at[iteration, f, me],
                dst_ref=arrived.at[iteration, f, me],
                send_sem=send_sem.at[0],
                recv_sem=recv_sem.at[iteration % 2, f],
                device_id={"region": peer},
                device_id_type=MESH,
            ).start()
            if between and n % GAP == GAP - 1:
                between.pop(0)()
        for part in between:
            part()

    maps.wait()
    columns.start()
    for f in bins:
        for i in range(row_blocks):
            target_ref[f, i : i + 1, :] = dirty_ref[f : f + 1, i * width : (i + 1) * width]

    for copy in first:
        copy.wait()
    flags.start()
    inverse, estimates, scaled = [], [], []
    for f in bins:
        diagonal = jnp.zeros((row_blocks, width), jnp.float32)
        for i in range(row_blocks):
            kept = jnp.zeros((strip, width), jnp.float32)
            for start in range(0, width, strip):
                piece = psf[f, i, 0, start : start + strip].astype(jnp.float32)
                kept = jnp.where(below == start, piece, kept)
            line = jnp.sum(kept, axis=0, keepdims=True)
            diagonal = jnp.where(row_ids == i, line, diagonal)
        target = target_ref[f]
        inv = 1.0 / diagonal
        estimate = jnp.maximum(0.0, target / diagonal)
        arrived[0, f, me] = estimate.astype(jnp.bfloat16)
        inverse.append(inv)
        scaled.append(target * inv)
        estimates.append(estimate)

    pl.semaphore_wait(barrier, regions - 1 + groups - 1)
    for f in bins:
        send(0, f)
    columns.wait()
    flags.wait()
    blocks_all = regions * row_blocks
    starts = [col_ref[0, k] for k in range(1, slots)]
    rest.wait()

    pairs = row_blocks // 2
    depths = (slots - 1) // 2

    def turn(row, carry):
        f, q = row // pairs, row % pairs
        for j in range(2):
            for k in range(slots - 1):
                rows = slice(k % 2 * width, k % 2 * width + width)
                alive = live_ref[2 * q + j, 1 + k].astype(jnp.float32)
                block = (psf[f, 2 * q + j, 1 + k].astype(jnp.float32) * alive).astype(jnp.bfloat16)
                turned[f, q, k // 2, rows, j * width : (j + 1) * width] = block.T
        return carry

    lax.fori_loop(0, freq_count * pairs, turn, 0)

    def near(accs, f, estimate):
        coarse = jnp.concatenate([estimate, jnp.zeros_like(estimate)], axis=0)
        coarse = jnp.concatenate([coarse, jnp.zeros_like(coarse)], axis=1).astype(jnp.bfloat16)
        for h in range(2):
            for m in range(2):
                i = 2 * (2 * m + h)
                side = [jnp.concatenate([psf[f, i + j, 0], psf[f, i + j, 1]], axis=0) for j in range(2)]
                pltpu.matmul_push_rhs(jnp.concatenate(side, axis=1), h, m)
        for h in range(2):
            for m in range(2):
                pltpu.matmul_acc_lhs(accs[f][m][h], coarse, h)

    nothing = jnp.zeros((2 * row_blocks, 2 * width), jnp.bfloat16)

    def ready(accs, f):
        def part(n, m):
            pltpu.matmul_push_rhs(turned[f, 2 * m, n], n // 2, m)
            if n == 0:
                pltpu.matmul_acc_lhs(accs[f][m][0], nothing, 0)

        return [functools.partial(part, n, m) for n in range(3) for m in range(2)]

    def multiply(accs, f, iteration):
        others = arrived.at[iteration, f, pl.ds(0, regions - 1)]
        pltpu.make_async_copy(others, others, recv_sem.at[iteration % 2, f]).wait()
        known = arrived[iteration, f].astype(jnp.float32).reshape(blocks_all, width)
        spread[f, :blocks_all] = known
        spread[f, blocks_all:] = known[:row_blocks]
        found = [spread[f, pl.ds(starts[k], row_blocks)] for k in range(slots - 1)]
        pad = jnp.zeros((row_blocks, 2 * width), jnp.float32)
        left = [
            jnp.concatenate([jnp.concatenate(found[2 * d : 2 * d + 2], axis=1), pad], axis=0).astype(jnp.bfloat16)
            for d in range(depths)
        ]
        for m in range(2):
            pltpu.matmul_acc_lhs(accs[f][m][0], left[0])
        for m in range(2):
            pltpu.matmul_acc_lhs(accs[f][m][0], left[1], 0)
            pltpu.matmul_push_rhs(turned[f, 2 * m + 1, 0], 0, m)
        for m in range(2):
            pltpu.matmul_acc_lhs(accs[f][m][0], left[2], 1)
            pltpu.matmul_push_rhs(turned[f, 2 * m + 1, 1], 1, m)
        for m in range(2):
            pltpu.matmul_acc_lhs(accs[f][m][1], left[0], 0)
            pltpu.matmul_push_rhs(turned[f, 2 * m + 1, 2], 0, m)
        for m in range(2):
            pltpu.matmul_acc_lhs(accs[f][m][1], left[1], 1)
        for m in range(2):
            pltpu.matmul_acc_lhs(accs[f][m][1], left[2], 0)
        applied = jnp.zeros((row_blocks, width), jnp.float32)
        for m in range(2):
            for h in range(2):
                product = pltpu.matmul_pop(accs[f][m][h])[:row_blocks]
                for j in range(2):
                    part = product[:, j * width : (j + 1) * width]
                    applied = jnp.where(row_ids == 2 * (2 * m + h) + j, part, applied)
        return applied

    shape = (2 * row_blocks, 2 * width)

    def sweep(iteration, estimates, last):
        def body(*refs):
            refs = list(refs)
            accs = [[[refs.pop(0) for h in range(2)] for m in range(2)] for f in bins]
            for f in bins:
                near(accs, f, estimates[f])
            nexts = []
            for part in ready(accs, 0):
                part()
            for f in bins:
                applied = multiply(accs, f, iteration)
                estimate = jnp.maximum(0.0, (estimates[f] + scaled[f]) - applied * inverse[f])
                nexts.append(estimate)
                coming = ready(accs, f + 1) if f + 1 < freq_count else []
                if last:
                    for part in coming:
                        part()
                else:
                    arrived[iteration + 1, f, me] = estimate.astype(jnp.bfloat16)
                    send(iteration + 1, f, coming)
            return tuple(nexts)

        return pl.run_scoped(
            body, *[pltpu.ACC(m)(shape, jnp.float32) for f in bins for m in range(2) for h in range(2)]
        )

    estimates = lax.fori_loop(0, ITERS - 1, functools.partial(sweep, last=False), tuple(estimates))
    estimates = sweep(ITERS - 1, estimates, last=True)
    local_sum = estimates[0]
    for f in bins[1:]:
        local_sum = local_sum + estimates[f]
    partial[group] = local_sum
    broad = []
    for step in range(1, groups):
        copy = pltpu.make_async_remote_copy(
            src_ref=partial.at[group],
            dst_ref=partial.at[group],
            send_sem=broad_send.at[step - 1],
            recv_sem=broad_recv.at[step - 1],
            device_id={"freq": lax.rem(group + step, groups)},
            device_id_type=MESH,
        )
        copy.start()
        broad.append(copy)
    for f in bins:
        for i in range(row_blocks):
            est_ref[f : f + 1, i * width : (i + 1) * width] = estimates[f][i : i + 1]
    others = arrived.at[:, :, pl.ds(0, regions - 1)]
    pltpu.make_async_copy(others, others, send_sem.at[0]).wait()
    for copy in broad:
        copy.wait()
    total = partial[0]
    for g in range(1, groups):
        total = total + partial[g]
    broad_ref[...] = total


def write_out(est_ref, broad_ref, est_out, broad_out, sems):
    copies = [
        pltpu.make_async_copy(est_ref, est_out, sems.at[0]),
        pltpu.make_async_copy(broad_ref, broad_out, sems.at[1]),
    ]
    for copy in copies:
        copy.start()
    for copy in copies:
        copy.wait()


def solution(mesh):
    regions, groups = mesh.shape["region"], mesh.shape["freq"]

    def local(dirty_map, psf_blocks, col_index, block_live):
        freq_count, row_blocks, slots, width, _ = psf_blocks.shape
        vmem = pl.BlockSpec(memory_space=pltpu.VMEM)
        anywhere = pl.BlockSpec(memory_space=pl.ANY)
        estimate, broadband = pl.pallas_call(
            functools.partial(kernel, regions, groups),
            out_shape=(
                pltpu.VMEM(dirty_map.shape, jnp.float32),
                pltpu.VMEM((row_blocks, width), jnp.float32),
            ),
            in_specs=[anywhere] * 4,
            out_specs=(vmem, vmem),
            scratch_shapes=[
                pltpu.VMEM(psf_blocks.shape, jnp.bfloat16),
                pltpu.VMEM((freq_count, row_blocks // 2, (slots - 1) // 2, 2 * width, 2 * width), jnp.bfloat16),
                pltpu.VMEM(dirty_map.shape, jnp.float32),
                pltpu.SMEM(col_index.shape, jnp.int32),
                pltpu.SMEM(block_live.shape, jnp.int32),
                pltpu.VMEM((freq_count, row_blocks, width), jnp.float32),
                pltpu.VMEM((ITERS, freq_count, regions, row_blocks, width), jnp.bfloat16),
                pltpu.VMEM((freq_count, (regions + 1) * row_blocks, width), jnp.float32),
                pltpu.VMEM((groups, row_blocks, width), jnp.float32),
                pltpu.SemaphoreType.DMA((2 + freq_count,)),
                pltpu.SemaphoreType.DMA((1,)),
                pltpu.SemaphoreType.DMA((2, freq_count)),
                pltpu.SemaphoreType.DMA((max(1, groups - 1),)),
                pltpu.SemaphoreType.DMA((max(1, groups - 1),)),
            ],
            compiler_params=pltpu.CompilerParams(collective_id=0, has_side_effects=True),
        )(dirty_map, psf_blocks, col_index, block_live)
        estimate, broadband = pl.pallas_call(
            write_out,
            out_shape=(
                jax.ShapeDtypeStruct(dirty_map.shape, jnp.float32),
                jax.ShapeDtypeStruct((row_blocks, width), jnp.float32),
            ),
            in_specs=[vmem, vmem],
            out_specs=(anywhere, anywhere),
            scratch_shapes=[pltpu.SemaphoreType.DMA((2,))],
        )(
            pltpu.with_memory_space_constraint(estimate, pltpu.VMEM),
            pltpu.with_memory_space_constraint(broadband, pltpu.VMEM),
        )
        return estimate, broadband.reshape(-1)

    return jax.shard_map(
        local,
        mesh=mesh,
        in_specs=(
            P("freq", "region"),
            P("freq", "region", None, None, None),
            P("region", None),
            P("region", None),
        ),
        out_specs=(P("freq", "region"), P("region")),
        check_vma=False,
    )
```

```python
import functools

import jax
import jax.numpy as jnp
from jax import lax
from jax.experimental import pallas as pl
from jax.experimental.pallas import tpu as pltpu
from jax.sharding import PartitionSpec as P

ITERS = 3
GAP = 2
MESH = pl.DeviceIdType.MESH


def partners(me, regions):
    if regions & (regions - 1):
        return [lax.rem(me + step, regions) for step in range(1, regions)]
    moves, bit = [], 1
    while bit < regions:
        moves.append(bit - 2 * bit * ((me // bit) % 2))
        bit *= 2
    masks = sorted(range(1, regions), key=lambda mask: (mask & 1, -mask))
    return [sum((move for n, move in enumerate(moves) if mask >> n & 1), me) for mask in masks]


def kernel(
    regions,
    groups,
    dirty_hbm,
    psf_hbm,
    col_hbm,
    live_hbm,
    est_ref,
    broad_ref,
    psf,
    turned,
    dirty_ref,
    col_ref,
    live_ref,
    target_ref,
    arrived,
    spread,
    partial,
    load_sem,
    send_sem,
    recv_sem,
    broad_recv,
):
    me = lax.axis_index("region")
    group = lax.axis_index("freq")
    peers = partners(me, regions)
    freq_count, row_blocks, slots, width = psf.shape[:4]
    bins = range(freq_count)

    maps = pltpu.make_async_copy(dirty_hbm, dirty_ref, load_sem.at[0])
    columns = pltpu.make_async_copy(col_hbm, col_ref, load_sem.at[0])
    flags = pltpu.make_async_copy(live_hbm, live_ref, load_sem.at[1])
    first = [
        pltpu.make_async_copy(psf_hbm.at[f, :, 0], psf.at[f, :, 0], load_sem.at[1 + f]) for f in bins
    ]
    rest = pltpu.make_async_copy(
        psf_hbm.at[:, :, pl.ds(1, slots - 1)],
        psf.at[:, :, pl.ds(1, slots - 1)],
        load_sem.at[1 + freq_count],
    )
    barrier = pltpu.get_barrier_semaphore()
    for peer in peers:
        pl.semaphore_signal(barrier, inc=1, device_id={"region": peer}, device_id_type=MESH)
    for step in range(1, groups):
        pl.semaphore_signal(
            barrier, inc=1, device_id={"freq": lax.rem(group + step, groups)}, device_id_type=MESH
        )
    for copy in first:
        copy.start()
    maps.start()
    rest.start()

    row_ids = lax.broadcasted_iota(jnp.int32, (row_blocks, width), 0)
    strip = 16
    below = lax.broadcasted_iota(jnp.int32, (strip, width), 1) - lax.broadcasted_iota(
        jnp.int32, (strip, width), 0
    )

    def send(iteration, f, between=()):
        between = list(between)
        for n, peer in enumerate(peers):
            pltpu.make_async_remote_copy(
                src_ref=arrived.at[iteration, f, me],
                dst_ref=arrived.at[iteration, f, me],
                send_sem=send_sem.at[0],
                recv_sem=recv_sem.at[iteration % 2, f],
                device_id={"region": peer},
                device_id_type=MESH,
            ).start()
            if between and n % GAP == GAP - 1:
                between.pop(0)()
        for part in between:
            part()

    maps.wait()
    columns.start()
    for f in bins:
        for i in range(row_blocks):
            target_ref[f, i : i + 1, :] = dirty_ref[f : f + 1, i * width : (i + 1) * width]

    for copy in first:
        copy.wait()
    flags.start()
    inverse, estimates, scaled = [], [], []
    for f in bins:
        diagonal = jnp.zeros((row_blocks, width), jnp.float32)
        for i in range(row_blocks):
            kept = jnp.zeros((strip, width), jnp.float32)
            for start in range(0, width, strip):
                piece = psf[f, i, 0, start : start + strip].astype(jnp.float32)
                kept = jnp.where(below == start, piece, kept)
            line = jnp.sum(kept, axis=0, keepdims=True)
            diagonal = jnp.where(row_ids == i, line, diagonal)
        target = target_ref[f]
        inv = 1.0 / diagonal
        estimate = jnp.maximum(0.0, target / diagonal)
        arrived[0, f, me] = estimate.astype(jnp.bfloat16)
        inverse.append(inv)
        scaled.append(target * inv)
        estimates.append(estimate)

    pl.semaphore_wait(barrier, regions - 1 + groups - 1)
    for f in bins:
        send(0, f)
    columns.wait()
    flags.wait()
    blocks_all = regions * row_blocks
    starts = [col_ref[0, k] for k in range(1, slots)]
    alive = [
        jnp.broadcast_to(live_ref[:, k : k + 1].astype(jnp.float32), (row_blocks, width))
        for k in range(1, slots)
    ]
    rest.wait()

    pairs = row_blocks // 2
    depths = (slots - 1) // 2

    def turn(row, carry):
        f, q = row // pairs, row % pairs
        for j in range(2):
            for k in range(slots - 1):
                rows = slice(k % 2 * width, k % 2 * width + width)
                turned[f, q, k // 2, rows, j * width : (j + 1) * width] = psf[f, 2 * q + j, 1 + k].T
        return carry

    lax.fori_loop(0, freq_count * pairs, turn, 0)

    def near(accs, f, estimate):
        coarse = jnp.concatenate([estimate, jnp.zeros_like(estimate)], axis=0)
        coarse = jnp.concatenate([coarse, jnp.zeros_like(coarse)], axis=1).astype(jnp.bfloat16)
        for h in range(2):
            for m in range(2):
                i = 2 * (2 * m + h)
                side = [jnp.concatenate([psf[f, i + j, 0], psf[f, i + j, 1]], axis=0) for j in range(2)]
                pltpu.matmul_push_rhs(jnp.concatenate(side, axis=1), h, m)
        for h in range(2):
            for m in range(2):
                pltpu.matmul_acc_lhs(accs[f][m][h], coarse, h)

    nothing = jnp.zeros((2 * row_blocks, 2 * width), jnp.bfloat16)

    def ready(accs, f):
        def part(n, m):
            pltpu.matmul_push_rhs(turned[f, 2 * m, n], n // 2, m)
            if n == 0:
                pltpu.matmul_acc_lhs(accs[f][m][0], nothing, 0)

        return [functools.partial(part, n, m) for n in range(3) for m in range(2)]

    def multiply(accs, f, iteration):
        others = arrived.at[iteration, f, pl.ds(0, regions - 1)]
        pltpu.make_async_copy(others, others, recv_sem.at[iteration % 2, f]).wait()
        known = arrived[iteration, f].astype(jnp.float32).reshape(blocks_all, width)
        spread[f, :blocks_all] = known
        spread[f, blocks_all:] = known[:row_blocks]
        found = [spread[f, pl.ds(starts[k], row_blocks)] * alive[k] for k in range(slots - 1)]
        pad = jnp.zeros((row_blocks, 2 * width), jnp.float32)
        left = [
            jnp.concatenate([jnp.concatenate(found[2 * d : 2 * d + 2], axis=1), pad], axis=0).astype(jnp.bfloat16)
            for d in range(depths)
        ]
        for m in range(2):
            pltpu.matmul_acc_lhs(accs[f][m][0], left[0])
        for m in range(2):
            pltpu.matmul_acc_lhs(accs[f][m][0], left[1], 0)
            pltpu.matmul_push_rhs(turned[f, 2 * m + 1, 0], 0, m)
        for m in range(2):
            pltpu.matmul_acc_lhs(accs[f][m][0], left[2], 1)
            pltpu.matmul_push_rhs(turned[f, 2 * m + 1, 1], 1, m)
        for m in range(2):
            pltpu.matmul_acc_lhs(accs[f][m][1], left[0], 0)
            pltpu.matmul_push_rhs(turned[f, 2 * m + 1, 2], 0, m)
        for m in range(2):
            pltpu.matmul_acc_lhs(accs[f][m][1], left[1], 1)
        for m in range(2):
            pltpu.matmul_acc_lhs(accs[f][m][1], left[2], 0)
        applied = jnp.zeros((row_blocks, width), jnp.float32)
        for m in range(2):
            for h in range(2):
                product = pltpu.matmul_pop(accs[f][m][h])[:row_blocks]
                for j in range(2):
                    part = product[:, j * width : (j + 1) * width]
                    applied = jnp.where(row_ids == 2 * (2 * m + h) + j, part, applied)
        return applied

    shape = (2 * row_blocks, 2 * width)

    def sweep(iteration, estimates, last):
        def body(*refs):
            refs = list(refs)
            accs = [[[refs.pop(0) for h in range(2)] for m in range(2)] for f in bins]
            for f in bins:
                near(accs, f, estimates[f])
            nexts = []
            for part in ready(accs, 0):
                part()
            for f in bins:
                applied = multiply(accs, f, iteration)
                estimate = jnp.maximum(0.0, (estimates[f] + scaled[f]) - applied * inverse[f])
                nexts.append(estimate)
                coming = ready(accs, f + 1) if f + 1 < freq_count else []
                if last:
                    for part in coming:
                        part()
                else:
                    arrived[iteration + 1, f, me] = estimate.astype(jnp.bfloat16)
                    send(iteration + 1, f, coming)
            return tuple(nexts)

        return pl.run_scoped(
            body, *[pltpu.ACC(m)(shape, jnp.float32) for f in bins for m in range(2) for h in range(2)]
        )

    estimates = lax.fori_loop(0, ITERS - 1, functools.partial(sweep, last=False), tuple(estimates))
    estimates = sweep(ITERS - 1, estimates, last=True)
    local_sum = estimates[0]
    for f in bins[1:]:
        local_sum = local_sum + estimates[f]
    partial[group] = local_sum
    broad = []
    for step in range(1, groups):
        copy = pltpu.make_async_remote_copy(
            src_ref=partial.at[group],
            dst_ref=partial.at[group],
            send_sem=load_sem.at[step - 1],
            recv_sem=broad_recv.at[step - 1],
            device_id={"freq": lax.rem(group + step, groups)},
            device_id_type=MESH,
        )
        copy.start()
        broad.append(copy)
    for f in bins:
        for i in range(row_blocks):
            est_ref[f : f + 1, i * width : (i + 1) * width] = estimates[f][i : i + 1]
    others = arrived.at[:, :, pl.ds(0, regions - 1)]
    pltpu.make_async_copy(others, others, send_sem.at[0]).wait()
    for copy in broad:
        copy.wait()
    total = partial[0]
    for g in range(1, groups):
        total = total + partial[g]
    broad_ref[...] = total


def write_out(est_ref, broad_ref, est_out, broad_out, sems):
    copies = [
        pltpu.make_async_copy(est_ref, est_out, sems.at[0]),
        pltpu.make_async_copy(broad_ref, broad_out, sems.at[1]),
    ]
    for copy in copies:
        copy.start()
    for copy in copies:
        copy.wait()


def solution(mesh):
    regions, groups = mesh.shape["region"], mesh.shape["freq"]

    def local(dirty_map, psf_blocks, col_index, block_live):
        freq_count, row_blocks, slots, width, _ = psf_blocks.shape
        vmem = pl.BlockSpec(memory_space=pltpu.VMEM)
        anywhere = pl.BlockSpec(memory_space=pl.ANY)
        estimate, broadband = pl.pallas_call(
            functools.partial(kernel, regions, groups),
            out_shape=(
                pltpu.VMEM(dirty_map.shape, jnp.float32),
                pltpu.VMEM((row_blocks, width), jnp.float32),
            ),
            in_specs=[anywhere] * 4,
            out_specs=(vmem, vmem),
            scratch_shapes=[
                pltpu.VMEM(psf_blocks.shape, jnp.bfloat16),
                pltpu.VMEM((freq_count, row_blocks // 2, (slots - 1) // 2, 2 * width, 2 * width), jnp.bfloat16),
                pltpu.VMEM(dirty_map.shape, jnp.float32),
                pltpu.SMEM(col_index.shape, jnp.int32),
                pltpu.VMEM(block_live.shape, jnp.int32),
                pltpu.VMEM((freq_count, row_blocks, width), jnp.float32),
                pltpu.VMEM((ITERS, freq_count, regions, row_blocks, width), jnp.bfloat16),
                pltpu.VMEM((freq_count, (regions + 1) * row_blocks, width), jnp.float32),
                pltpu.VMEM((groups, row_blocks, width), jnp.float32),
                pltpu.SemaphoreType.DMA((max(2 + freq_count, groups - 1),)),
                pltpu.SemaphoreType.DMA((1,)),
                pltpu.SemaphoreType.DMA((2, freq_count)),
                pltpu.SemaphoreType.DMA((max(1, groups - 1),)),
            ],
            compiler_params=pltpu.CompilerParams(collective_id=0, has_side_effects=True),
        )(dirty_map, psf_blocks, col_index, block_live)
        estimate, broadband = pl.pallas_call(
            write_out,
            out_shape=(
                jax.ShapeDtypeStruct(dirty_map.shape, jnp.float32),
                jax.ShapeDtypeStruct((row_blocks, width), jnp.float32),
            ),
            in_specs=[vmem, vmem],
            out_specs=(anywhere, anywhere),
            scratch_shapes=[pltpu.SemaphoreType.DMA((2,))],
        )(
            pltpu.with_memory_space_constraint(estimate, pltpu.VMEM),
            pltpu.with_memory_space_constraint(broadband, pltpu.VMEM),
        )
        return estimate, broadband.reshape(-1)

    return jax.shard_map(
        local,
        mesh=mesh,
        in_specs=(
            P("freq", "region"),
            P("freq", "region", None, None, None),
            P("region", None),
            P("region", None),
        ),
        out_specs=(P("freq", "region"), P("region")),
        check_vma=False,
    )
```
